32 devices in a mesh: row: 8 (over z, core), col: 4 (over y, x).
Axes of the slice: x: 2, y: 2, z: 4, core: 2. Of those that a mesh axis runs over, the one named last changes fastest.
Arguments:
- matrix: float32 [2048, 2048], P('row', 'col'), may hold values from -6 to 6
- pivots: int32 [3, 256], replicated, may hold values from 0 to 2047, as said below
- inverses: float32 [3, 256, 256], replicated, may hold values from -0.0234375 to 0.0234375
Outputs:
- factored: float32 [2048, 2048], P('row', 'col')
The draws below stay inside these ranges and needn't reach their ends.
Inputs may be any that keep to these rules, and one draw needn't show every extreme that they name: For panel k and position i, pivots[k, i] is either k * 256 + i or a row of index (k + 1) * 256 or more; position 0 of every panel is k * 256; no row is named twice within one panel; every panel names row 2047.
All inputs are finite; a program needn't handle non-finite values.
Results may differ from the reference program's by a relative error of at most 0.00017.
Values sent between devices are 32-bit elements; how exact they have to be, the bound alone decides.
No kernel may reach another device: no remote copies, remote signals or barrier semaphores. Data moves between devices by JAX's collectives and lax.ppermute only.
A program may use at most 64 MiB of HBM per device.

```python
import jax
import jax.numpy as jnp
from jax import lax

NB = 256
R_DEV = 256
C_DEV = 512
PANELS = 3
ROWS = 2048
COLS = 2048
N_ROW = 8
N_COL = 4


def draw_pivots(key, part):
    panels = []
    offsets = jnp.arange(NB, dtype=jnp.int32)
    for panel in range(PANELS):
        subkey = jax.random.fold_in(key, 11 + panel)
        key_perm, key_spot, key_stay = jax.random.split(subkey, 3)
        start = (panel + 1) * NB
        count = ROWS - start - 1
        picks = jax.random.permutation(key_perm, count)[:NB].astype(jnp.int32) + start
        spot = jax.random.randint(key_spot, (), 1, NB)
        picks = jnp.where(offsets == spot, ROWS - 1, picks)
        stay = ((jax.random.randint(key_stay, (NB,), 0, 4) == 0) | (offsets == 0)) & (offsets != spot)
        panels.append(jnp.where(stay, panel * NB + offsets, picks).astype(jnp.int32))
    return jnp.stack(panels)


def levels(rng, dims, cuts, low, high):
    gain = 1.0
    for axis_at, shards_of in cuts:
        draws = jax.random.uniform(jax.random.fold_in(jax.random.fold_in(rng, 6), axis_at), (shards_of,), jnp.float32, low / len(cuts), high / len(cuts))
        gain = gain * jnp.repeat(jnp.exp(draws), dims[axis_at] // shards_of).reshape((-1,) + (1,) * (len(dims) - 1 - axis_at))
    return gain


def normal_values(key, dims, spread, most, pieces=(), kind=jnp.bfloat16):
    values = spread * jax.random.normal(key, dims, jnp.float32)
    if pieces:
        values = values * levels(key, dims, pieces, -0.22, 0.18)
    return jnp.clip(values, -most, most).astype(kind)


def setup_inputs(seed: int = 0) -> dict:
    key_of = jax.random.split(jax.random.key(seed), 4)
    return {
        "matrix": normal_values(key_of[0], (ROWS, COLS), 1.0, 6.0, ((0, 8), (1, 4)), jnp.float32),
        "pivots": draw_pivots(jax.random.fold_in(key_of[3], 71), 0),
        "inverses": normal_values(key_of[2], (PANELS, NB, NB), (NB * NB) ** -0.5, 0.0234375, (), jnp.float32),
    }


def to_logical(stored):
    row_blocks = R_DEV // NB
    col_blocks = C_DEV // NB
    shaped = stored.reshape(N_ROW, row_blocks, NB, N_COL, col_blocks, NB)
    return shaped.transpose(1, 0, 2, 4, 3, 5).reshape(ROWS, COLS)


def to_stored(logical):
    row_blocks = R_DEV // NB
    col_blocks = C_DEV // NB
    shaped = logical.reshape(row_blocks, N_ROW, NB, col_blocks, N_COL, NB)
    return shaped.transpose(1, 0, 2, 4, 3, 5).reshape(ROWS, COLS)


def reference(matrix, pivots, inverses):
    grid = to_logical(matrix)
    offsets = jnp.arange(NB, dtype=jnp.int32)
    for panel in range(PANELS):
        top = panel * NB
        chosen = pivots[panel]
        tops = top + offsets
        stay = chosen == tops
        upper = grid[chosen]
        displaced = grid[top:top + NB]
        grid = grid.at[jnp.where(stay, tops, chosen)].set(displaced)
        grid = grid.at[top:top + NB].set(upper)
        lower = top + NB
        strip = grid[lower:, top:top + NB]
        factor = jnp.dot(strip, inverses[panel], precision=lax.Precision.HIGHEST, preferred_element_type=jnp.float32)
        grid = grid.at[lower:, top:top + NB].set(factor)
        urow = grid[top:top + NB, lower:]
        trailing = grid[lower:, lower:] - jnp.dot(factor, urow, precision=lax.Precision.HIGHEST, preferred_element_type=jnp.float32)
        grid = grid.at[lower:, lower:].set(trailing)
    return to_stored(grid)
```

```python
import jax
import jax.numpy as jnp
from jax import lax
from jax.sharding import PartitionSpec as P


def dot(a, b):
    return jnp.dot(a, b, precision=lax.Precision.HIGH, preferred_element_type=jnp.float32)


def swap(array, axis, distance):
    return lax.ppermute(array, axis, [(i, i ^ distance) for i in range(lax.axis_size(axis))])


def distances(size):
    return [1 << k for k in reversed(range(size.bit_length() - 1))]


def spread(array, axis, order):
    held = {0: array}
    for distance in order:
        held.update({slot ^ distance: swap(held[slot], axis, distance) for slot in list(held)})
    return [held[slot] for slot in range(len(held))]


def on_device(matrix, pivots, inverses):
    rows_here, cols_here = matrix.shape
    panels, block = pivots.shape
    nrow = lax.axis_size("row")
    ncol = lax.axis_size("col")
    rank_row = lax.axis_index("row")
    rank_col = lax.axis_index("col")
    offsets = jnp.arange(block, dtype=jnp.int32)

    def before(panel, rows):
        hit = rows[:, None] == pivots[panel][None, :]
        moved = jnp.sum(jnp.where(hit, panel * block + offsets[None, :], 0), axis=1)
        return jnp.where(jnp.any(hit, axis=1), moved, rows)

    def first(panel, rows):
        for earlier in reversed(range(panel)):
            rows = before(earlier, rows)
        return rows

    def place(rows):
        owner = rows // block % nrow
        return (owner ^ rank_row) * rows_here + rows // block // nrow * block + rows % block

    tops = [first(panel, pivots[panel]) for panel in range(panels)]
    local = jnp.arange(rows_here, dtype=jnp.int32)
    own = (local // block * nrow + rank_row) * block + local % block
    own_from = first(panels, own)
    for panel in range(panels):
        own_from = own_from.at[:block].set(
            jnp.where(rank_row == panel, tops[panel], own_from[:block])
        )
    core = rank_row % 2
    other = jnp.where(core == 0, jnp.where(rank_col == 0, 1, 0), jnp.where(rank_col == 2, 1, 2))
    other_from = jnp.where(other == 0, tops[0], jnp.where(other == 1, tops[1], tops[2]))

    table_a = jnp.concatenate(spread(matrix[:, :block], "row", distances(nrow)))
    table_b = jnp.concatenate(spread(matrix[:, block:], "row", distances(nrow)))

    sent = table_a[place(jnp.concatenate([own_from, other_from]))]
    half = sent.shape[0] // 2
    here = [
        jnp.concatenate(pair)
        for pair in zip(
            spread(sent[:half], "col", distances(ncol)),
            spread(sent[half:], "col", distances(ncol)[::-1]),
        )
    ]

    def of_panel(pieces, panel):
        picked = pieces[0]
        for slot in range(1, ncol):
            picked = jnp.where((panel ^ rank_col) == slot, pieces[slot], picked)
        return picked

    column = [of_panel(here, panel) for panel in range(panels)]
    mine = [c[rows_here:] for c in column]
    theirs = [swap(m, "row", 1) for m in mine]
    low = [jnp.where(core == 0, m, t) for m, t in zip(mine, theirs)]
    high = [jnp.where(core == 0, t, m) for m, t in zip(mine, theirs)]
    raw = [c[:rows_here] for c in column]

    wanted = jnp.concatenate(tops + [own_from])
    wide = jnp.concatenate([table_a[place(wanted)], table_b[place(wanted)]], axis=1)
    upper = [wide[k * block : (k + 1) * block] for k in range(panels)]
    current = wide[panels * block :]

    u01, u02 = low[1], low[2]
    l10 = dot(low[0], inverses[0])
    l20 = dot(high[0], inverses[0])
    l21 = dot(high[1] - dot(l20, u01), inverses[1])
    u12 = high[2] - dot(l10, u02)
    l0 = jnp.where(rank_row > 0, dot(raw[0], inverses[0]), 0.0)
    l1 = jnp.where(rank_row > 1, dot(raw[1] - dot(l0, u01), inverses[1]), 0.0)
    l2 = jnp.where(rank_row > 2, dot(raw[2] - dot(l0, u02) - dot(l1, u12), inverses[2]), 0.0)

    upper[1] = upper[1] - dot(l10, upper[0])
    upper[2] = upper[2] - dot(l20, upper[0]) - dot(l21, upper[1])
    gblock = jnp.arange(cols_here, dtype=jnp.int32) // block * ncol + rank_col
    masked = [jnp.where((gblock > k)[None, :], upper[k], 0.0) for k in range(panels)]
    result = current - dot(jnp.concatenate([l0, l1, l2], axis=1), jnp.concatenate(masked))
    head = result[:, :block]
    for k, factor in enumerate([l0, l1, l2]):
        head = jnp.where((rank_col == k) & (rank_row > k), factor, head)
    return jnp.concatenate([head, result[:, block:]], axis=1)


def solution(mesh):
    placed = (P("row", "col"), P(), P())
    return jax.shard_map(
        on_device, mesh=mesh, in_specs=placed, out_specs=P("row", "col"), check_vma=False
    )
```

```python
import jax
import jax.numpy as jnp
from jax import lax
from jax.experimental import pallas as pl
from jax.experimental.pallas import tpu as pltpu
from jax.sharding import PartitionSpec as P


VMEM = pl.BlockSpec(memory_space=pltpu.VMEM)
SMEM = pl.BlockSpec(memory_space=pltpu.SMEM)
PARAMS = pltpu.CompilerParams(vmem_limit_bytes=16 << 20)


def swap(array, axis, distance):
    return lax.ppermute(array, axis, [(i, i ^ distance) for i in range(lax.axis_size(axis))])


def distances(size):
    return [1 << k for k in reversed(range(size.bit_length() - 1))]


def spread(array, axis, order):
    held = {0: array}
    for distance in order:
        held.update({slot ^ distance: swap(held[slot], axis, distance) for slot in list(held)})
    return [held[slot] for slot in range(len(held))]


def pick_rows(slots, rows, outs):
    height, width = slots[0].shape
    total = sum(outs)

    def kernel(rows_ref, *refs):
        slot_refs = refs[: len(slots)]
        out_refs = refs[len(slots) : -1]
        table = refs[-1]
        for s, ref in enumerate(slot_refs):
            table[s * height : (s + 1) * height, :] = ref[...]
        base = 0
        for out_ref, count in zip(out_refs, outs):

            def body(i, carry, out_ref=out_ref, base=base):
                for u in range(8):
                    j = i * 8 + u
                    out_ref[pl.ds(j, 1), :] = table[pl.ds(rows_ref[base + j], 1), :]
                return carry

            lax.fori_loop(0, count // 8, body, 0)
            base += count

    moved = total * width * 4
    return pl.pallas_call(
        kernel,
        out_shape=[jax.ShapeDtypeStruct((n, width), slots[0].dtype) for n in outs],
        in_specs=[SMEM] + [VMEM] * len(slots),
        out_specs=[VMEM] * len(outs),
        scratch_shapes=[pltpu.VMEM((len(slots) * height, width), slots[0].dtype)],
        compiler_params=PARAMS,
        cost_estimate=pl.CostEstimate(flops=0, bytes_accessed=2 * moved, transcendentals=0),
    )(rows, *slots)


def split(x):
    high = x.astype(jnp.bfloat16)
    return high, (x - high.astype(jnp.float32)).astype(jnp.bfloat16)


def product(a, b):
    def one(x, y):
        return jnp.dot(x, y, preferred_element_type=jnp.float32)

    return one(a[0], b[0]) + (one(a[0], b[1]) + one(a[1], b[0]))


def eliminate(ranks, raw, mine, theirs, inverses, top_wide, own_wide, ncol):
    panels, block = inverses.shape[:2]
    rows_here = raw[0].shape[0]
    pieces = len(own_wide)
    width = own_wide[0].shape[1]
    nslot = len(raw)

    def kernel(ranks_ref, inv_ref, *refs):
        raw_refs = refs[:nslot]
        mine_refs = refs[nslot : 2 * nslot]
        theirs_refs = refs[2 * nslot : 3 * nslot]
        top_refs = refs[3 * nslot : 3 * nslot + pieces * panels]
        own_refs = refs[3 * nslot + pieces * panels : 3 * nslot + pieces * (panels + 1)]
        out_ref, strip, square = refs[3 * nslot + pieces * (panels + 1) :]
        rank_row = ranks_ref[0]
        rank_col = ranks_ref[1]
        core = ranks_ref[2]
        for slot in range(nslot):
            panel = rank_col ^ slot

            @pl.when(panel < panels)
            def _(slot=slot, panel=panel):
                strip[panel] = raw_refs[slot][...]
                square[panel, core] = mine_refs[slot][...]
                square[panel, 1 - core] = theirs_refs[slot][...]

        inv = [split(inv_ref[k]) for k in range(panels)]
        below = [jnp.where(rank_row > k, 1.0, 0.0) for k in range(panels)]
        u01 = split(square[1, 0])
        u02 = split(square[2, 0])
        a21 = square[1, 1]
        a12 = square[2, 1]
        l10 = split(product(split(square[0, 0]), inv[0]))
        l20 = split(product(split(square[0, 1]), inv[0]))
        l0_full = product(split(strip[0]), inv[0]) * below[0]
        l0 = split(l0_full)
        l21 = split(product(split(a21 - product(l20, u01)), inv[1]))
        u12 = split(a12 - product(l10, u02))
        l1_full = product(split(strip[1] - product(l0, u01)), inv[1]) * below[1]
        l1 = split(l1_full)
        rest = strip[2] - product(l0, u02) - product(l1, u12)
        l2_full = product(split(rest), inv[2]) * below[2]
        l2 = split(l2_full)
        full = [l0_full, l1_full, l2_full]
        for piece in range(pieces):
            gblock = piece * ncol + rank_col
            keep = [jnp.where(gblock > k, 1.0, 0.0) for k in range(panels)]
            top = [top_refs[piece * panels + k][...] for k in range(panels)]
            u0 = split(top[0])
            u1_full = top[1] - product(l10, u0)
            u1 = split(u1_full)
            u2 = split(top[2] - product(l20, u0) - product(l21, u1))
            result = own_refs[piece][...]
            for k, (factor, u) in enumerate(zip([l0, l1, l2], [u0, u1, u2])):
                term = product(factor, u)
                result = result - (term * keep[k] if piece * ncol <= k else term)
            if piece == 0:
                for k in range(panels):
                    replace = jnp.logical_and(gblock == k, rank_row > k)
                    result = jnp.where(replace, full[k], result)
            out_ref[:, piece * width : (piece + 1) * width] = result

    flops = 2 * 24 * 3 * block**3
    return pl.pallas_call(
        kernel,
        out_shape=jax.ShapeDtypeStruct((rows_here, width * pieces), jnp.float32),
        in_specs=[SMEM] + [VMEM] * (1 + 3 * nslot + pieces * (panels + 1)),
        out_specs=VMEM,
        scratch_shapes=[
            pltpu.VMEM((panels, rows_here, block), jnp.float32),
            pltpu.VMEM((panels, 2, block, block), jnp.float32),
        ],
        compiler_params=PARAMS,
        cost_estimate=pl.CostEstimate(flops=flops, bytes_accessed=8 << 20, transcendentals=0),
    )(ranks, inverses, *raw, *mine, *theirs, *top_wide, *own_wide)


def on_device(matrix, pivots, inverses):
    rows_here, cols_here = matrix.shape
    panels, block = pivots.shape
    nrow = lax.axis_size("row")
    ncol = lax.axis_size("col")
    rank_row = lax.axis_index("row")
    rank_col = lax.axis_index("col")
    offsets = jnp.arange(block, dtype=jnp.int32)

    def before(panel, rows):
        hit = rows[:, None] == pivots[panel][None, :]
        moved = jnp.sum(jnp.where(hit, panel * block + offsets[None, :], 0), axis=1)
        return jnp.where(jnp.any(hit, axis=1), moved, rows)

    def first(panel, rows):
        for earlier in reversed(range(panel)):
            rows = before(earlier, rows)
        return rows

    def place(rows):
        owner = rows // block % nrow
        return (owner ^ rank_row) * rows_here + rows // block // nrow * block + rows % block

    tops = [first(panel, pivots[panel]) for panel in range(panels)]
    local = jnp.arange(rows_here, dtype=jnp.int32)
    own = (local // block * nrow + rank_row) * block + local % block
    own_from = first(panels, own)
    for panel in range(panels):
        own_from = own_from.at[:block].set(
            jnp.where(rank_row == panel, tops[panel], own_from[:block])
        )
    core = rank_row % 2
    other = jnp.where(core == 0, jnp.where(rank_col == 0, 1, 0), jnp.where(rank_col == 2, 1, 2))
    other_from = jnp.where(other == 0, tops[0], jnp.where(other == 1, tops[1], tops[2]))
    sent_from = place(jnp.concatenate([own_from, other_from]))
    wanted = place(jnp.concatenate(tops + [own_from]))

    slots = [spread(matrix[:, :block], "row", distances(nrow))]
    for at in range(block, cols_here, block):
        slots.append(spread(matrix[:, at : at + block], "row", distances(nrow)))

    own_rows, other_rows = pick_rows(slots[0], sent_from, [rows_here, block])
    mine = spread(other_rows, "col", distances(ncol)[::-1])
    raw = spread(own_rows, "col", distances(ncol))
    theirs = [swap(m, "row", 1) for m in mine]

    wide = [pick_rows(s, wanted, [block] * panels + [rows_here]) for s in slots]
    top_wide = [t for w in wide for t in w[:panels]]
    own_wide = [w[panels] for w in wide]
    ranks = jnp.stack([rank_row, rank_col, core]).astype(jnp.int32)
    return eliminate(ranks, raw, mine, theirs, inverses, top_wide, own_wide, ncol)


def solution(mesh):
    placed = (P("row", "col"), P(), P())
    return jax.shard_map(
        on_device, mesh=mesh, in_specs=placed, out_specs=P("row", "col"), check_vma=False
    )
```

```python
import jax
import jax.numpy as jnp
from jax import lax
from jax.experimental import pallas as pl
from jax.experimental.pallas import tpu as pltpu
from jax.sharding import PartitionSpec as P


VMEM = pl.BlockSpec(memory_space=pltpu.VMEM)
CUTS = [128, 128]
SMEM = pl.BlockSpec(memory_space=pltpu.SMEM)
PARAMS = pltpu.CompilerParams(vmem_limit_bytes=16 << 20)


def swap(array, axis, distance):
    return lax.ppermute(array, axis, [(i, i ^ distance) for i in range(lax.axis_size(axis))])


def distances(size):
    return [1 << k for k in reversed(range(size.bit_length() - 1))]


def spread(array, axis, order):
    held = {0: array}
    for distance in order:
        for slot in list(held):
            held[slot ^ distance] = swap(held[slot], axis, distance)
    return [held.get(slot) for slot in range(max(held) + 1)]


def relayed(array, height, axis, straight):
    held = [(array, array[height:], None)]
    upper, lower = {}, {}
    for slot in range(1, lax.axis_size(axis)):
        low = slot & -slot
        high = 1 << (slot.bit_length() - 1)
        if low == high:
            whole = swap(array, axis, slot)
            upper[slot], lower[slot] = whole[:height], whole[height:]
            held.append((whole, lower[slot], None))
        else:
            if straight:
                lower[slot] = swap(array[height:], axis, slot)
            else:
                lower[slot] = swap(lower[slot ^ high], axis, high)
            upper[slot] = swap(upper[slot ^ low], axis, low)
            held.append((None, lower[slot], upper[slot]))
    return held


def stack(arrays):
    height, width = arrays[0].shape

    def kernel(*refs):
        for i, ref in enumerate(refs[:-1]):
            refs[-1][i * height : (i + 1) * height, :] = ref[...]

    return pl.pallas_call(
        kernel,
        out_shape=jax.ShapeDtypeStruct((height * len(arrays), width), arrays[0].dtype),
        in_specs=[VMEM] * len(arrays),
        out_specs=VMEM,
        compiler_params=PARAMS,
        cost_estimate=pl.CostEstimate(flops=0, bytes_accessed=1 << 20, transcendentals=0),
    )(*arrays)


def pick_rest(slots, rows, shared, rows_here):
    height, width = slots[0].shape
    count = shared + rows_here

    def kernel(rows_ref, *refs):
        slot_refs = refs[: len(slots)]
        kept, sent, table = refs[len(slots) :]
        for s, ref in enumerate(slot_refs):
            table[s * height : (s + 1) * height, :] = ref[...]

        def copy(target, first, base, total):
            def body(i, carry):
                found = [table[pl.ds(rows_ref[base + i * 32 + u], 1), :] for u in range(32)]
                for u in range(32):
                    target[pl.ds(first + i * 32 + u, 1), :] = found[u]
                return carry

            lax.fori_loop(0, total // 32, body, 0)

        copy(kept, 0, 0, count)
        copy(sent, shared, count, rows_here)
        sent[:shared, :] = kept[:shared, :]

    moved = 2 * count * width * 4
    shape = jax.ShapeDtypeStruct((count, width), slots[0].dtype)
    return pl.pallas_call(
        kernel,
        out_shape=[shape, shape],
        in_specs=[SMEM] + [VMEM] * len(slots),
        out_specs=[VMEM, VMEM],
        scratch_shapes=[pltpu.VMEM((len(slots) * height, width), slots[0].dtype)],
        compiler_params=PARAMS,
        cost_estimate=pl.CostEstimate(flops=0, bytes_accessed=2 * moved, transcendentals=0),
    )(rows, *slots)


def pick_rows(slots, rows, outs, height, width):
    total = sum(outs)

    def kernel(rows_ref, *refs):
        slot_refs = refs[: len(slots)]
        out_refs = refs[len(slots) : -1]
        table = refs[-1]
        for s, (ref, (_, row, column)) in enumerate(zip(slot_refs, slots)):
            found = ref[row : row + height, column : column + width]
            table[s * height : (s + 1) * height, :] = found
        base = 0
        for out_ref, count in zip(out_refs, outs):

            def body(i, carry, out_ref=out_ref, base=base):
                found = [table[pl.ds(rows_ref[base + i * 32 + u], 1), :] for u in range(32)]
                for u in range(32):
                    out_ref[pl.ds(i * 32 + u, 1), :] = found[u]
                return carry

            lax.fori_loop(0, count // 32, body, 0)
            base += count

    moved = total * width * 4
    kind = slots[0][0].dtype
    return pl.pallas_call(
        kernel,
        out_shape=[jax.ShapeDtypeStruct((n, width), kind) for n in outs],
        in_specs=[SMEM] + [VMEM] * len(slots),
        out_specs=[VMEM] * len(outs),
        scratch_shapes=[pltpu.VMEM((len(slots) * height, width), kind)],
        compiler_params=PARAMS,
        cost_estimate=pl.CostEstimate(flops=0, bytes_accessed=2 * moved, transcendentals=0),
    )(rows, *[array for array, _, _ in slots])


def split(x):
    high = x.astype(jnp.bfloat16)
    return high, (x - high.astype(jnp.float32)).astype(jnp.bfloat16)


def product(a, b):
    def one(x, y):
        return jnp.dot(x, y, preferred_element_type=jnp.float32)

    return one(a[0], b[0]) + (one(a[0], b[1]) + one(a[1], b[0]))


def eliminate(ranks, here, theirs, inverses, wide, rest, cols_here, ncol):
    panels, block = inverses.shape[:2]
    nslot = len(here[0])
    rows_here = here[0][0][0].shape[0] - block
    flat, where = [], {}
    for part in range(len(here)):
        for slot, (whole, lower, upper) in enumerate(here[part]):
            arrays = [whole] if upper is None else [upper, lower]
            where[part, slot] = len(flat), len(arrays)
            flat.extend(arrays)
    given = [array for array, _ in theirs]
    source = {key: (len(flat) + i, n * block) for i, (_, keys) in enumerate(theirs) for n, key in enumerate(keys)}
    flat.extend(given)
    flat_wide = [array for part in wide for array in part] + list(rest)
    half = rest[0].shape[1] if rest else 0
    rows_rest = panels * block + rows_here

    def kernel(ranks_ref, inv_ref, *refs):
        strip_refs = refs[: len(flat)]
        wide_refs = refs[len(flat) : len(flat) + len(flat_wide)]
        out_ref, strip, square, table = refs[len(flat) + len(flat_wide) :]
        rank_row = ranks_ref[0]
        rank_col = ranks_ref[1]
        core = ranks_ref[2]
        inv = [split(inv_ref[k]) for k in range(panels)]
        for slot in range(nslot):
            panel = jnp.minimum(rank_col ^ slot, panels)
            at = 0
            for part in range(len(here)):
                width = here[part][0][0].shape[1]
                columns = slice(at, at + width)
                at += width
                place, count = where[part, slot]
                found = strip_refs[place : place + count]
                first = rows_here if count == 1 else 0
                index, row = source[part, slot]
                strip[panel, :, columns] = found[0][:rows_here, :]
                square[2 * panel + core, :, columns] = found[-1][first : first + block, :]
                square[2 * panel + 1 - core, :, columns] = strip_refs[index][row : row + block, :]
        if rest:
            table[core] = wide_refs[-2][...]
            table[1 - core] = wide_refs[-1][...]

        def columns_of(rows, piece):
            if piece == 0:
                if rows == panels:
                    parts = [strip_refs[where[part, 0][0]][:rows_here, :] for part in range(len(here))]
                else:
                    parts = [wide_refs[part * panels + rows][...] for part in range(len(here))]
                return jnp.concatenate(parts, axis=1)
            taken = slice(rows * block, rows_rest if rows == panels else (rows + 1) * block)
            start, parts = (piece - 1) * block, []
            while start < piece * block:
                stop = min(piece * block, (start // half + 1) * half)
                parts.append(table[start // half, taken, start % half : start % half + stop - start])
                start = stop
            return jnp.concatenate(parts, axis=1)

        pieces = range(cols_here // block)
        below = [jnp.where(rank_row > k, 1.0, 0.0) for k in range(panels)]
        u01 = split(square[2])
        u02 = split(square[4])
        l10 = split(product(split(square[0]), inv[0]))
        l20 = split(product(split(square[1]), inv[0]))
        full = [product(split(strip[0]), inv[0]) * below[0]]
        factor = [split(full[0])]
        top = [[split(columns_of(0, piece)) for piece in pieces]]
        l21 = split(product(split(square[3] - product(l20, u01)), inv[1]))
        half1 = split(strip[1] - product(factor[0], u01))
        u12 = split(square[5] - product(l10, u02))
        full.append(product(half1, inv[1]) * below[1])
        factor.append(split(full[1]))
        top.append([split(columns_of(1, p) - product(l10, top[0][p])) for p in pieces])
        half2 = split(strip[2] - product(factor[0], u02) - product(factor[1], u12))
        top.append(
            [
                split(columns_of(2, p) - product(l20, top[0][p]) - product(l21, top[1][p]))
                for p in pieces
            ]
        )
        full.append(product(half2, inv[2]) * below[2])
        factor.append(split(full[2]))
        for piece in pieces:
            gblock = piece * ncol + rank_col
            result = columns_of(panels, piece)
            for k in range(panels):
                term = product(factor[k], top[k][piece])
                keep = jnp.where(gblock > k, 1.0, 0.0)
                result = result - (term * keep if piece * ncol <= k else term)
            if piece == 0:
                for k in range(panels):
                    replace = jnp.logical_and(gblock == k, rank_row > k)
                    result = jnp.where(replace, full[k], result)
            out_ref[:, piece * block : (piece + 1) * block] = result

    flops = 2 * 24 * 3 * block**3
    return pl.pallas_call(
        kernel,
        out_shape=jax.ShapeDtypeStruct((rows_here, cols_here), jnp.float32),
        in_specs=[SMEM] + [VMEM] * (1 + len(flat) + len(flat_wide)),
        out_specs=VMEM,
        scratch_shapes=[
            pltpu.VMEM((panels + 1, rows_here, block), jnp.float32),
            pltpu.VMEM((2 * panels + 2, block, block), jnp.float32),
            pltpu.VMEM((2, rows_rest, max(half, 128)), jnp.float32),
        ],
        compiler_params=PARAMS,
        cost_estimate=pl.CostEstimate(flops=flops, bytes_accessed=8 << 20, transcendentals=0),
    )(ranks, inverses, *flat, *flat_wide)


def on_device(matrix, pivots, inverses):
    rows_here, cols_here = matrix.shape
    panels, block = pivots.shape
    nrow = lax.axis_size("row")
    ncol = lax.axis_size("col")
    rank_row = lax.axis_index("row")
    rank_col = lax.axis_index("col")
    offsets = jnp.arange(block, dtype=jnp.int32)

    def before(panel, rows):
        hit = rows[:, None] == pivots[panel][None, :]
        moved = jnp.sum(jnp.where(hit, panel * block + offsets[None, :], 0), axis=1)
        return jnp.where(jnp.any(hit, axis=1), moved, rows)

    def first(panel, rows):
        for earlier in reversed(range(panel)):
            rows = before(earlier, rows)
        return rows

    def place(rows):
        owner = rows // block % nrow
        return (owner ^ rank_row) * rows_here + rows // block // nrow * block + rows % block

    tops = [first(panel, pivots[panel]) for panel in range(panels)]
    core = rank_row % 2

    def taken(rank):
        local = jnp.arange(rows_here, dtype=jnp.int32)
        rows = first(panels, (local // block * nrow + rank) * block + local % block)
        for panel in range(panels):
            rows = rows.at[:block].set(jnp.where(rank == panel, tops[panel], rows[:block]))
        return rows

    own_from = taken(rank_row)
    other = jnp.where(core == 0, jnp.where(rank_col == 0, 1, 0), jnp.where(rank_col == 2, 1, 2))
    other_from = jnp.where(other == 0, tops[0], jnp.where(other == 1, tops[1], tops[2]))
    sent_from = place(jnp.concatenate([own_from, other_from]))
    wanted = place(jnp.concatenate(tops + [own_from, taken(rank_row ^ 1)]))

    starts = [sum(CUTS[:i]) for i in range(len(CUTS))]
    beside = swap(matrix, "row", 1)
    own_parts = [matrix[:, at : at + width] for at, width in zip(starts, CUTS)]
    slots = []
    for part, array in enumerate(own_parts):
        held = spread(array, "row", distances(nrow)[:-1])[::2]
        pairs = [(array, 0, 0), (beside, 0, starts[part])]
        for slot in range(1, len(held)):
            pairs += [(held[slot], 0, 0), (swap(held[slot], "row", 1), 0, 0)]
        slots.append(pairs)
    half = (cols_here - block) // 2
    rest = []
    if half:
        source = lax.optimization_barrier((matrix, wanted))[0]
        both = [
            jnp.where(core == 0, x[:, block : block + half], x[:, block + half :])
            for x in (source, beside)
        ]
        both = spread(jnp.concatenate(both), "row", distances(nrow)[:-1])
        rest, sent = pick_rest(both[::2], wanted, panels * block, rows_here)
        rest = [rest, swap(sent, "row", 1)]
    here, wide = [], []
    for part, width in enumerate(CUTS):
        (sent,) = pick_rows(slots[part], sent_from, [rows_here + block], rows_here, width)
        here.append(relayed(sent, rows_here, "col", part == len(CUTS) - 1))
    for part, width in enumerate(CUTS):
        wide.append(pick_rows(slots[part], wanted, [block] * panels, rows_here, width))
    slot_of = range(1, ncol)
    near_slots = [0] + [slot for slot in slot_of if slot & (slot - 1) == 0]
    far_slots = [slot for slot in slot_of if slot & (slot - 1)]
    last = len(CUTS) - 1
    turns = [
        [(part, slot) for part in range(last) for slot in near_slots] + [(last, 0)],
        [(part, slot) for part in range(last) for slot in far_slots]
        + [(last, slot) for slot in near_slots[1:] + far_slots],
    ]
    theirs = []
    for keys in turns:
        arrays = [here[part][slot][1] for part, slot in keys]
        merged = stack(arrays) if len(arrays) > 1 else arrays[0]
        theirs.append((swap(merged, "row", 1), keys))
    ranks = jnp.stack([rank_row, rank_col, core]).astype(jnp.int32)
    return eliminate(ranks, here, theirs, inverses, wide, rest, cols_here, ncol)


def solution(mesh):
    placed = (P("row", "col"), P(), P())
    return jax.shard_map(on_device, mesh=mesh, in_specs=placed, out_specs=P("row", "col"), check_vma=False)
```

```python
import jax
import jax.numpy as jnp
from jax import lax
from jax.experimental import pallas as pl
from jax.experimental.pallas import tpu as pltpu
from jax.sharding import PartitionSpec as P


VMEM = pl.BlockSpec(memory_space=pltpu.VMEM)
CUTS = [128, 128]
SMEM = pl.BlockSpec(memory_space=pltpu.SMEM)
PARAMS = pltpu.CompilerParams(vmem_limit_bytes=16 << 20)


def swap(array, axis, distance):
    return lax.ppermute(array, axis, [(i, i ^ distance) for i in range(lax.axis_size(axis))])


def distances(size):
    return [1 << k for k in reversed(range(size.bit_length() - 1))]


def spread(array, axis, order):
    held = {0: array}
    for distance in order:
        for slot in list(held):
            held[slot ^ distance] = swap(held[slot], axis, distance)
    return [held.get(slot) for slot in range(max(held) + 1)]


def relayed(array, height, axis, straight):
    held = [(array, array[height:], None)]
    upper, lower = {}, {}
    for slot in range(1, lax.axis_size(axis)):
        low = slot & -slot
        high = 1 << (slot.bit_length() - 1)
        if low == high:
            whole = swap(array, axis, slot)
            upper[slot], lower[slot] = whole[:height], whole[height:]
            held.append((whole, lower[slot], None))
        else:
            if straight:
                lower[slot] = swap(array[height:], axis, slot)
            else:
                lower[slot] = swap(lower[slot ^ high], axis, high)
            upper[slot] = swap(upper[slot ^ low], axis, low)
            held.append((None, lower[slot], upper[slot]))
    return held


def stack(arrays):
    height, width = arrays[0].shape

    def kernel(*refs):
        for i, ref in enumerate(refs[:-1]):
            refs[-1][i * height : (i + 1) * height, :] = ref[...]

    return pl.pallas_call(
        kernel,
        out_shape=jax.ShapeDtypeStruct((height * len(arrays), width), arrays[0].dtype),
        in_specs=[VMEM] * len(arrays),
        out_specs=VMEM,
        compiler_params=PARAMS,
        cost_estimate=pl.CostEstimate(flops=0, bytes_accessed=1 << 20, transcendentals=0),
    )(*arrays)


def pick_rest(slots, rows, shared, rows_here):
    height, width = slots[0].shape
    count = shared + rows_here

    def kernel(rows_ref, *refs):
        slot_refs = refs[: len(slots)]
        kept, sent, table = refs[len(slots) :]
        for s, ref in enumerate(slot_refs):
            table[s * height : (s + 1) * height, :] = ref[...]

        def copy(target, first, base, total):
            def body(i, carry):
                found = [table[pl.ds(rows_ref[base + i * 32 + u], 1), :] for u in range(32)]
                for u in range(32):
                    target[pl.ds(first + i * 32 + u, 1), :] = found[u]
                return carry

            lax.fori_loop(0, total // 32, body, 0)

        copy(kept, 0, 0, count)
        copy(sent, shared, count, rows_here)
        sent[:shared, :] = kept[:shared, :]

    moved = 2 * count * width * 4
    shape = jax.ShapeDtypeStruct((count, width), slots[0].dtype)
    return pl.pallas_call(
        kernel,
        out_shape=[shape, shape],
        in_specs=[SMEM] + [VMEM] * len(slots),
        out_specs=[VMEM, VMEM],
        scratch_shapes=[pltpu.VMEM((len(slots) * height, width), slots[0].dtype)],
        compiler_params=PARAMS,
        cost_estimate=pl.CostEstimate(flops=0, bytes_accessed=2 * moved, transcendentals=0),
    )(rows, *slots)


def pick_rows(slots, rows, outs, height, width):
    total = sum(outs)

    def kernel(rows_ref, *refs):
        slot_refs = refs[: len(slots)]
        out_refs = refs[len(slots) : -1]
        table = refs[-1]
        for s, (ref, (_, row, column)) in enumerate(zip(slot_refs, slots)):
            found = ref[row : row + height, column : column + width]
            table[s * height : (s + 1) * height, :] = found
        base = 0
        for out_ref, count in zip(out_refs, outs):

            def body(i, carry, out_ref=out_ref, base=base):
                found = [table[pl.ds(rows_ref[base + i * 32 + u], 1), :] for u in range(32)]
                for u in range(32):
                    out_ref[pl.ds(i * 32 + u, 1), :] = found[u]
                return carry

            lax.fori_loop(0, count // 32, body, 0)
            base += count

    moved = total * width * 4
    kind = slots[0][0].dtype
    return pl.pallas_call(
        kernel,
        out_shape=[jax.ShapeDtypeStruct((n, width), kind) for n in outs],
        in_specs=[SMEM] + [VMEM] * len(slots),
        out_specs=[VMEM] * len(outs),
        scratch_shapes=[pltpu.VMEM((len(slots) * height, width), kind)],
        compiler_params=PARAMS,
        cost_estimate=pl.CostEstimate(flops=0, bytes_accessed=2 * moved, transcendentals=0),
    )(rows, *[array for array, _, _ in slots])


def split(x):
    high = x.astype(jnp.bfloat16)
    return high, (x - high.astype(jnp.float32)).astype(jnp.bfloat16)


def product(a, b):
    def one(x, y):
        return jnp.dot(x, y, preferred_element_type=jnp.float32)

    return one(a[0], b[0]) + one(a[0], b[1]) + one(a[1], b[0])


def eliminate(ranks, here, theirs, inverses, wide, rest, cols_here, ncol):
    panels, block = inverses.shape[:2]
    nslot = len(here[0])
    rows_here = here[0][0][0].shape[0] - block
    flat, where = [], {}
    for part in range(len(here)):
        for slot, (whole, lower, upper) in enumerate(here[part]):
            arrays = [whole] if upper is None else [upper, lower]
            where[part, slot] = len(flat), len(arrays)
            flat.extend(arrays)
    given = [array for array, _ in theirs]
    source = {key: (len(flat) + i, n * block) for i, (_, keys) in enumerate(theirs) for n, key in enumerate(keys)}
    flat.extend(given)
    flat_wide = [array for part in wide for array in part] + list(rest)
    half = rest[0].shape[1] if rest else 0
    rows_rest = panels * block + rows_here

    def kernel(ranks_ref, inv_ref, *refs):
        strip_refs = refs[: len(flat)]
        wide_refs = refs[len(flat) : len(flat) + len(flat_wide)]
        out_ref, strip, square = refs[len(flat) + len(flat_wide) :]
        rank_row = ranks_ref[0]
        rank_col = ranks_ref[1]
        core = ranks_ref[2]
        inv = [split(inv_ref[k]) for k in range(panels)]
        for slot in range(nslot):
            panel = jnp.minimum(rank_col ^ slot, panels)
            at = 0
            for part in range(len(here)):
                width = here[part][0][0].shape[1]
                columns = slice(at, at + width)
                at += width
                place, count = where[part, slot]
                found = strip_refs[place : place + count]
                first = rows_here if count == 1 else 0
                index, row = source[part, slot]
                strip[panel, :, columns] = found[0][:rows_here, :]
                square[2 * panel + core, :, columns] = found[-1][first : first + block, :]
                square[2 * panel + 1 - core, :, columns] = strip_refs[index][row : row + block, :]

        def columns_of(rows, piece):
            if piece == 0:
                if rows == panels:
                    parts = [strip_refs[where[part, 0][0]][:rows_here, :] for part in range(len(here))]
                else:
                    parts = [wide_refs[part * panels + rows][...] for part in range(len(here))]
                return jnp.concatenate(parts, axis=1)
            taken = slice(rows * block, rows_rest if rows == panels else (rows + 1) * block)
            start, parts = (piece - 1) * block, []
            while start < piece * block:
                stop = min(piece * block, (start // half + 1) * half)
                inside = slice(start % half, start % half + stop - start)
                one, two = wide_refs[-2][taken, inside], wide_refs[-1][taken, inside]
                parts.append(jnp.where(core == start // half, one, two))
                start = stop
            return jnp.concatenate(parts, axis=1)

        pieces = range(cols_here // block)
        below = [jnp.where(rank_row > k, 1.0, 0.0) for k in range(panels)]

        def part_of(piece):
            return slice(piece * block, (piece + 1) * block)

        def subtract(k):
            for piece in pieces:
                held = columns_of(panels, piece) if k == 0 else out_ref[:, part_of(piece)]
                term = product(factor[k], top[k][piece])
                if piece * ncol <= k:
                    term = term * jnp.where(piece * ncol + rank_col > k, 1.0, 0.0)
                out_ref[:, part_of(piece)] = held - term

        u01 = split(square[2])
        u02 = split(square[4])
        full = [product(split(strip[0]), inv[0]) * below[0]]
        l20 = split(product(split(square[1]), inv[0]))
        l10 = split(product(split(square[0]), inv[0]))
        factor = [split(full[0])]
        half1 = split(strip[1] - product(factor[0], u01))
        half21 = split(square[3] - product(l20, u01))
        top = [[split(columns_of(0, piece)) for piece in pieces]]
        u12 = split(square[5] - product(l10, u02))
        full.append(product(half1, inv[1]) * below[1])
        l21 = split(product(half21, inv[1]))
        top.append([split(columns_of(1, p) - product(l10, top[0][p])) for p in pieces])
        factor.append(split(full[1]))
        half2 = strip[2] - product(factor[0], u02)
        subtract(0)
        half2 = split(half2 - product(factor[1], u12))
        top.append(
            [
                split(columns_of(2, p) - product(l20, top[0][p]) - product(l21, top[1][p]))
                for p in pieces
            ]
        )
        full.append(product(half2, inv[2]) * below[2])
        subtract(1)
        factor.append(split(full[2]))
        subtract(2)
        for k in range(panels):

            @pl.when(jnp.logical_and(rank_col == k, rank_row > k))
            def _(k=k):
                out_ref[:, part_of(0)] = full[k]

    flops = 2 * 24 * 3 * block**3
    return pl.pallas_call(
        kernel,
        out_shape=jax.ShapeDtypeStruct((rows_here, cols_here), jnp.float32),
        in_specs=[SMEM] + [VMEM] * (1 + len(flat) + len(flat_wide)),
        out_specs=VMEM,
        scratch_shapes=[
            pltpu.VMEM((panels + 1, rows_here, block), jnp.float32),
            pltpu.VMEM((2 * panels + 2, block, block), jnp.float32),
        ],
        compiler_params=PARAMS,
        cost_estimate=pl.CostEstimate(flops=flops, bytes_accessed=8 << 20, transcendentals=0),
    )(ranks, inverses, *flat, *flat_wide)


def on_device(matrix, pivots, inverses):
    rows_here, cols_here = matrix.shape
    panels, block = pivots.shape
    nrow = lax.axis_size("row")
    ncol = lax.axis_size("col")
    rank_row = lax.axis_index("row")
    rank_col = lax.axis_index("col")
    offsets = jnp.arange(block, dtype=jnp.int32)

    def before(panel, rows):
        hit = rows[:, None] == pivots[panel][None, :]
        moved = jnp.sum(jnp.where(hit, panel * block + offsets[None, :], 0), axis=1)
        return jnp.where(jnp.any(hit, axis=1), moved, rows)

    def first(panel, rows):
        for earlier in reversed(range(panel)):
            rows = before(earlier, rows)
        return rows

    def place(rows):
        owner = rows // block % nrow
        return (owner ^ rank_row) * rows_here + rows // block // nrow * block + rows % block

    tops = [first(panel, pivots[panel]) for panel in range(panels)]
    core = rank_row % 2

    def taken(rank):
        local = jnp.arange(rows_here, dtype=jnp.int32)
        rows = first(panels, (local // block * nrow + rank) * block + local % block)
        for panel in range(panels):
            rows = rows.at[:block].set(jnp.where(rank == panel, tops[panel], rows[:block]))
        return rows

    own_from = taken(rank_row)
    other = jnp.where(core == 0, jnp.where(rank_col == 0, 1, 0), jnp.where(rank_col == 2, 1, 2))
    other_from = jnp.where(other == 0, tops[0], jnp.where(other == 1, tops[1], tops[2]))
    sent_from = place(jnp.concatenate([own_from, other_from]))
    wanted = place(jnp.concatenate(tops + [own_from, taken(rank_row ^ 1)]))

    starts = [sum(CUTS[:i]) for i in range(len(CUTS))]
    beside = swap(matrix, "row", 1)
    own_parts = [matrix[:, at : at + width] for at, width in zip(starts, CUTS)]
    slots = []
    for part, array in enumerate(own_parts):
        held = spread(array, "row", distances(nrow)[:-1])[::2]
        pairs = [(array, 0, 0), (beside, 0, starts[part])]
        for slot in range(1, len(held)):
            pairs += [(held[slot], 0, 0), (swap(held[slot], "row", 1), 0, 0)]
        slots.append(pairs)
    half = (cols_here - block) // 2
    rest = []
    if half:
        source = lax.optimization_barrier((matrix, wanted))[0]
        both = [
            jnp.where(core == 0, x[:, block : block + half], x[:, block + half :])
            for x in (source, beside)
        ]
        both = spread(jnp.concatenate(both), "row", distances(nrow)[:-1])
        rest, sent = pick_rest(both[::2], wanted, panels * block, rows_here)
        rest = [rest, swap(sent, "row", 1)]
    here, wide = [], []
    for part, width in enumerate(CUTS):
        (sent,) = pick_rows(slots[part], sent_from, [rows_here + block], rows_here, width)
        here.append(relayed(sent, rows_here, "col", part == len(CUTS) - 1))
    for part, width in enumerate(CUTS):
        wide.append(pick_rows(slots[part], wanted, [block] * panels, rows_here, width))
    slot_of = range(1, ncol)
    near_slots = [0] + [slot for slot in slot_of if slot & (slot - 1) == 0]
    far_slots = [slot for slot in slot_of if slot & (slot - 1)]
    last = len(CUTS) - 1
    turns = [
        [(part, slot) for part in range(last) for slot in near_slots] + [(last, 0)],
        [(part, slot) for part in range(last) for slot in far_slots]
        + [(last, slot) for slot in near_slots[1:] + far_slots],
    ]
    theirs = []
    for keys in turns:
        arrays = [here[part][slot][1] for part, slot in keys]
        merged = stack(arrays) if len(arrays) > 1 else arrays[0]
        theirs.append((swap(merged, "row", 1), keys))
    ranks = jnp.stack([rank_row, rank_col, core]).astype(jnp.int32)
    return eliminate(ranks, here, theirs, inverses, wide, rest, cols_here, ncol)


def solution(mesh):
    placed = (P("row", "col"), P(), P())
    return jax.shard_map(
        on_device, mesh=mesh, in_specs=placed, out_specs=P("row", "col"), check_vma=False
    )
```

```python
import jax
import jax.numpy as jnp
from jax import lax
from jax.experimental import pallas as pl
from jax.experimental.pallas import tpu as pltpu
from jax.sharding import PartitionSpec as P


VMEM = pl.BlockSpec(memory_space=pltpu.VMEM)
CUTS = [128, 128]
SMEM = pl.BlockSpec(memory_space=pltpu.SMEM)
PARAMS = pltpu.CompilerParams(vmem_limit_bytes=16 << 20)


def swap(array, axis, distance):
    return lax.ppermute(array, axis, [(i, i ^ distance) for i in range(lax.axis_size(axis))])


def distances(size):
    return [1 << k for k in reversed(range(size.bit_length() - 1))]


def spread(array, axis, order):
    held = {0: array}
    for distance in order:
        for slot in list(held):
            held[slot ^ distance] = swap(held[slot], axis, distance)
    return [held.get(slot) for slot in range(max(held) + 1)]


def relayed(array, height, axis, straight):
    held = [(array, array[height:], None)]
    upper, lower = {}, {}
    for slot in range(1, lax.axis_size(axis)):
        low = slot & -slot
        high = 1 << (slot.bit_length() - 1)
        if low == high:
            whole = swap(array, axis, slot)
            upper[slot], lower[slot] = whole[:height], whole[height:]
            held.append((whole, lower[slot], None))
        else:
            if straight:
                lower[slot] = swap(array[height:], axis, slot)
            else:
                lower[slot] = swap(lower[slot ^ high], axis, high)
            upper[slot] = swap(upper[slot ^ low], axis, low)
            held.append((None, lower[slot], upper[slot]))
    return held


def stack(arrays):
    height, width = arrays[0].shape

    def kernel(*refs):
        for i, ref in enumerate(refs[:-1]):
            refs[-1][i * height : (i + 1) * height, :] = ref[...]

    return pl.pallas_call(
        kernel,
        out_shape=jax.ShapeDtypeStruct((height * len(arrays), width), arrays[0].dtype),
        in_specs=[VMEM] * len(arrays),
        out_specs=VMEM,
        compiler_params=PARAMS,
        cost_estimate=pl.CostEstimate(flops=0, bytes_accessed=1 << 20, transcendentals=0),
    )(*arrays)


def pick_rest(slots, rows, shared, rows_here):
    height, width = slots[0].shape
    count = shared + rows_here

    def kernel(rows_ref, *refs):
        slot_refs = refs[: len(slots)]
        kept, sent, table = refs[len(slots) :]
        for s, ref in enumerate(slot_refs):
            table[s * height : (s + 1) * height, :] = ref[...]

        def copy(target, first, base, total):
            def body(i, carry):
                found = [table[pl.ds(rows_ref[base + i * 64 + u], 1), :] for u in range(64)]
                for u in range(64):
                    target[pl.ds(first + i * 64 + u, 1), :] = found[u]
                return carry

            lax.fori_loop(0, total // 64, body, 0)

        copy(kept, 0, 0, count)
        copy(sent, shared, count, rows_here)
        sent[:shared, :] = kept[:shared, :]

    moved = 2 * count * width * 4
    shape = jax.ShapeDtypeStruct((count, width), slots[0].dtype)
    return pl.pallas_call(
        kernel,
        out_shape=[shape, shape],
        in_specs=[SMEM] + [VMEM] * len(slots),
        out_specs=[VMEM, VMEM],
        scratch_shapes=[pltpu.VMEM((len(slots) * height, width), slots[0].dtype)],
        compiler_params=PARAMS,
        cost_estimate=pl.CostEstimate(flops=0, bytes_accessed=2 * moved, transcendentals=0),
    )(rows, *slots)


def pick_rows(slots, rows, outs, height, width):
    total = sum(outs)

    def kernel(rows_ref, *refs):
        slot_refs = refs[: len(slots)]
        out_refs = refs[len(slots) : -1]
        table = refs[-1]
        for s, (ref, (_, row, column)) in enumerate(zip(slot_refs, slots)):
            found = ref[row : row + height, column : column + width]
            table[s * height : (s + 1) * height, :] = found
        base = 0
        for out_ref, count in zip(out_refs, outs):

            def body(i, carry, out_ref=out_ref, base=base):
                found = [table[pl.ds(rows_ref[base + i * 64 + u], 1), :] for u in range(64)]
                for u in range(64):
                    out_ref[pl.ds(i * 64 + u, 1), :] = found[u]
                return carry

            lax.fori_loop(0, count // 64, body, 0)
            base += count

    moved = total * width * 4
    kind = slots[0][0].dtype
    return pl.pallas_call(
        kernel,
        out_shape=[jax.ShapeDtypeStruct((n, width), kind) for n in outs],
        in_specs=[SMEM] + [VMEM] * len(slots),
        out_specs=[VMEM] * len(outs),
        scratch_shapes=[pltpu.VMEM((len(slots) * height, width), kind)],
        compiler_params=PARAMS,
        cost_estimate=pl.CostEstimate(flops=0, bytes_accessed=2 * moved, transcendentals=0),
    )(rows, *[array for array, _, _ in slots])


def split(x):
    high = x.astype(jnp.bfloat16)
    return high, (x - high.astype(jnp.float32)).astype(jnp.bfloat16)


def product(a, b):
    def one(x, y):
        return jnp.dot(x, y, preferred_element_type=jnp.float32)

    return one(a[0], b[0]) + one(a[0], b[1]) + one(a[1], b[0])


def eliminate(ranks, here, theirs, inverses, wide, rest, cols_here, ncol):
    panels, block = inverses.shape[:2]
    nslot = len(here[0])
    rows_here = here[0][0][0].shape[0] - block
    flat, where = [], {}
    for part in range(len(here)):
        for slot, (whole, lower, upper) in enumerate(here[part]):
            arrays = [whole] if upper is None else [upper, lower]
            where[part, slot] = len(flat), len(arrays)
            flat.extend(arrays)
    given = [array for array, _ in theirs]
    source = {key: (len(flat) + i, n * block) for i, (_, keys) in enumerate(theirs) for n, key in enumerate(keys)}
    flat.extend(given)
    flat_wide = [array for part in wide for array in part] + list(rest)
    half = rest[0].shape[1] if rest else 0
    rows_rest = panels * block + rows_here

    def kernel(ranks_ref, inv_ref, *refs):
        strip_refs = refs[: len(flat)]
        wide_refs = refs[len(flat) : len(flat) + len(flat_wide)]
        out_ref, strip, square = refs[len(flat) + len(flat_wide) :]
        rank_row = ranks_ref[0]
        rank_col = ranks_ref[1]
        core = ranks_ref[2]
        inv = [split(inv_ref[k]) for k in range(panels)]
        for slot in range(nslot):
            panel = jnp.minimum(rank_col ^ slot, panels)
            at = 0
            for part in range(len(here)):
                width = here[part][0][0].shape[1]
                columns = slice(at, at + width)
                at += width
                place, count = where[part, slot]
                found = strip_refs[place : place + count]
                first = rows_here if count == 1 else 0
                index, row = source[part, slot]
                strip[panel, :, columns] = found[0][:rows_here, :]
                square[2 * panel + core, :, columns] = found[-1][first : first + block, :]
                square[2 * panel + 1 - core, :, columns] = strip_refs[index][row : row + block, :]

        def columns_of(rows, piece):
            if piece == 0:
                if rows == panels:
                    parts = [strip_refs[where[part, 0][0]][:rows_here, :] for part in range(len(here))]
                else:
                    parts = [wide_refs[part * panels + rows][...] for part in range(len(here))]
                return jnp.concatenate(parts, axis=1)
            taken = slice(rows * block, rows_rest if rows == panels else (rows + 1) * block)
            start, parts = (piece - 1) * block, []
            while start < piece * block:
                stop = min(piece * block, (start // half + 1) * half)
                inside = slice(start % half, start % half + stop - start)
                one, two = wide_refs[-2][taken, inside], wide_refs[-1][taken, inside]
                parts.append(jnp.where(core == start // half, one, two))
                start = stop
            return jnp.concatenate(parts, axis=1)

        pieces = range(cols_here // block)
        below = [jnp.where(rank_row > k, 1.0, 0.0) for k in range(panels)]

        def part_of(piece):
            return slice(piece * block, (piece + 1) * block)

        def subtract(k):
            for piece in pieces:
                held = columns_of(panels, piece) if k == 0 else out_ref[:, part_of(piece)]
                term = product(factor[k], top[k][piece])
                if piece * ncol <= k:
                    term = term * jnp.where(piece * ncol + rank_col > k, 1.0, 0.0)
                out_ref[:, part_of(piece)] = held - term

        u01 = split(square[2])
        u02 = split(square[4])
        full = [product(split(strip[0]), inv[0]) * below[0]]
        l20 = split(product(split(square[1]), inv[0]))
        l10 = split(product(split(square[0]), inv[0]))
        factor = [split(full[0])]
        half1 = split(strip[1] - product(factor[0], u01))
        half21 = split(square[3] - product(l20, u01))
        top = [[split(columns_of(0, piece)) for piece in pieces]]
        u12 = split(square[5] - product(l10, u02))
        full.append(product(half1, inv[1]) * below[1])
        l21 = split(product(half21, inv[1]))
        top.append([split(columns_of(1, p) - product(l10, top[0][p])) for p in pieces])
        factor.append(split(full[1]))
        half2 = strip[2] - product(factor[0], u02)
        subtract(0)
        half2 = split(half2 - product(factor[1], u12))
        top.append(
            [
                split(columns_of(2, p) - product(l20, top[0][p]) - product(l21, top[1][p]))
                for p in pieces
            ]
        )
        full.append(product(half2, inv[2]) * below[2])
        subtract(1)
        factor.append(split(full[2]))
        subtract(2)
        for k in range(panels):

            @pl.when(jnp.logical_and(rank_col == k, rank_row > k))
            def _(k=k):
                out_ref[:, part_of(0)] = full[k]

    flops = 2 * 24 * 3 * block**3
    return pl.pallas_call(
        kernel,
        out_shape=jax.ShapeDtypeStruct((rows_here, cols_here), jnp.float32),
        in_specs=[SMEM] + [VMEM] * (1 + len(flat) + len(flat_wide)),
        out_specs=VMEM,
        scratch_shapes=[
            pltpu.VMEM((panels + 1, rows_here, block), jnp.float32),
            pltpu.VMEM((2 * panels + 2, block, block), jnp.float32),
        ],
        compiler_params=PARAMS,
        cost_estimate=pl.CostEstimate(flops=flops, bytes_accessed=8 << 20, transcendentals=0),
    )(ranks, inverses, *flat, *flat_wide)


def on_device(matrix, pivots, inverses):
    rows_here, cols_here = matrix.shape
    panels, block = pivots.shape
    nrow = lax.axis_size("row")
    ncol = lax.axis_size("col")
    rank_row = lax.axis_index("row")
    rank_col = lax.axis_index("col")
    offsets = jnp.arange(block, dtype=jnp.int32)

    def before(panel, rows):
        hit = rows[:, None] == pivots[panel][None, :]
        moved = jnp.sum(jnp.where(hit, panel * block + offsets[None, :], 0), axis=1)
        return jnp.where(jnp.any(hit, axis=1), moved, rows)

    def first(panel, rows):
        for earlier in reversed(range(panel)):
            rows = before(earlier, rows)
        return rows

    def place(rows):
        owner = rows // block % nrow
        return (owner ^ rank_row) * rows_here + rows // block // nrow * block + rows % block

    tops = [first(panel, pivots[panel]) for panel in range(panels)]
    core = rank_row % 2

    def taken(rank):
        local = jnp.arange(rows_here, dtype=jnp.int32)
        rows = first(panels, (local // block * nrow + rank) * block + local % block)
        for panel in range(panels):
            rows = rows.at[:block].set(jnp.where(rank == panel, tops[panel], rows[:block]))
        return rows

    own_from = taken(rank_row)
    other = jnp.where(core == 0, jnp.where(rank_col == 0, 1, 0), jnp.where(rank_col == 2, 1, 2))
    other_from = jnp.where(other == 0, tops[0], jnp.where(other == 1, tops[1], tops[2]))
    sent_from = place(jnp.concatenate([own_from, other_from]))
    wanted = place(jnp.concatenate(tops + [own_from, taken(rank_row ^ 1)]))

    starts = [sum(CUTS[:i]) for i in range(len(CUTS))]
    beside = swap(matrix, "row", 1)
    own_parts = [matrix[:, at : at + width] for at, width in zip(starts, CUTS)]
    slots = []
    for part, array in enumerate(own_parts):
        held = spread(array, "row", distances(nrow)[:-1])[::2]
        pairs = [(array, 0, 0), (beside, 0, starts[part])]
        for slot in range(1, len(held)):
            pairs += [(held[slot], 0, 0), (swap(held[slot], "row", 1), 0, 0)]
        slots.append(pairs)
    half = (cols_here - block) // 2
    rest = []
    if half:
        source = lax.optimization_barrier((matrix, wanted))[0]
        both = [
            jnp.where(core == 0, x[:, block : block + half], x[:, block + half :])
            for x in (source, beside)
        ]
        both = spread(jnp.concatenate(both), "row", distances(nrow)[:-1])
        rest, sent = pick_rest(both[::2], wanted, panels * block, rows_here)
        rest = [rest, swap(sent, "row", 1)]
    here, wide = [], []
    for part, width in enumerate(CUTS):
        (sent,) = pick_rows(slots[part], sent_from, [rows_here + block], rows_here, width)
        here.append(relayed(sent, rows_here, "col", part == len(CUTS) - 1))
    for part, width in enumerate(CUTS):
        wide.append(pick_rows(slots[part], wanted, [block] * panels, rows_here, width))
    slot_of = range(1, ncol)
    near_slots = [0] + [slot for slot in slot_of if slot & (slot - 1) == 0]
    far_slots = [slot for slot in slot_of if slot & (slot - 1)]
    last = len(CUTS) - 1
    turns = [
        [(part, slot) for part in range(last) for slot in near_slots] + [(last, 0)],
        [(part, slot) for part in range(last) for slot in far_slots]
        + [(last, slot) for slot in near_slots[1:] + far_slots],
    ]
    theirs = []
    for keys in turns:
        arrays = [here[part][slot][1] for part, slot in keys]
        merged = stack(arrays) if len(arrays) > 1 else arrays[0]
        theirs.append((swap(merged, "row", 1), keys))
    ranks = jnp.stack([rank_row, rank_col, core]).astype(jnp.int32)
    return eliminate(ranks, here, theirs, inverses, wide, rest, cols_here, ncol)


def solution(mesh):
    placed = (P("row", "col"), P(), P())
    return jax.shard_map(
        on_device, mesh=mesh, in_specs=placed, out_specs=P("row", "col"), check_vma=False
    )
```
